32 devices in a mesh: sec: 8 (over y, x, core), mpo: 4 (over z).
Axes of the slice: x: 2, y: 2, z: 4, core: 2. Of those that a mesh axis runs over, the one named last changes fastest.
Arguments:
- guess: float32 [6144, 256], P('sec'), may hold values from -6 to 6
- left_env: bfloat16 [20, 6144, 768], P('mpo', 'sec'), may hold values from -0.21875 to 0.21875
- right_env: bfloat16 [20, 2048, 256], P('mpo', 'sec'), may hold values from -0.375 to 0.375
- block_rows: int32 [8], replicated, may hold values from 1 to 768, 2048 in all
- charges: int32 [20], P('mpo'), may hold values from -2 to 2, as said below
- ranks: int32 [8], replicated, may hold values from 1 to 256
Outputs:
- wavefunction: float32 [6144, 256], P(('sec', 'mpo'))
- truncated: float32 [6144, 256], P(('sec', 'mpo'))
The draws below stay inside these ranges and needn't reach their ends.
Inputs may be any that keep to these rules, and one draw needn't show every extreme that they name: The 5 terms of one index of mpo (each aligned run of 5 terms) carry the charges -2, -1, 0, 1, 2 once each.
All inputs are finite; a program needn't handle non-finite values.
Results may differ from the reference program's by a relative error of at most 0.01.
Values may be sent and summed in bfloat16 or wider, within the bound.
A program may use at most 64 MiB of HBM per device.

```python
import math
import jax
import jax.numpy as jnp
import numpy as np
from jax import lax

MEAN = 256
RB = 256
ITERS = 4
CAP = 768
NSEC = 8
TERMS = 20


def draw_charges(key, part):
    subkeys = jax.random.split(jax.random.fold_in(key, 7), TERMS // 5)
    groups = jax.vmap(lambda subkey: jax.random.permutation(subkey, 5))(subkeys)
    return (groups.reshape(-1) - 2).astype(jnp.int32)


def place_ends(array, key, least, largest):
    place = [jax.random.randint(jax.random.fold_in(key, axis), (), 0, length) for axis, length in enumerate(array.shape)]
    main_axis = array.shape.index(max(array.shape))
    beside = place[:main_axis] + [(place[main_axis] + 1) % array.shape[main_axis]] + place[main_axis + 1:]
    return array.at[tuple(place)].set(least).at[tuple(beside)].set(largest)


def block_levels(rng, dims, pieces, smallest, largest):
    def one(position, shards_of):
        steps = jax.random.uniform(jax.random.fold_in(jax.random.fold_in(rng, 6), position), (shards_of,), jnp.float32, smallest / len(pieces), largest / len(pieces))
        return jnp.repeat(jnp.exp(steps), dims[position] // shards_of).reshape((-1,) + (1,) * (len(dims) - position - 1))

    gain = one(*pieces[0])
    for cut in pieces[1:]:
        gain = gain * one(*cut)
    return gain


def length_profile(amount, total, most, skew):
    loads = [(1 << 20) // math.isqrt(rank ** skew) + 1 for rank in range(2, amount + 1)]
    rest, given = total - most - (amount - 1), [1] * (amount - 1)
    while rest > 0:
        free = [i for i in range(amount - 1) if given[i] < most]
        whole, remaining = sum([loads[i] for i in free]), rest
        for i in free:
            addition = min(most - given[i], max(1, remaining * loads[i] // whole), rest)
            given[i] = given[i] + addition
            rest = rest - addition
    return np.array([most] + given)


def ragged(stream_key, amount, total, most, lean):
    if amount == 2:
        one = jax.random.randint(stream_key, (), max(1, total - most), min(most, total - 1) + 1)
        return jnp.stack([one, total - one])
    tallies = jnp.asarray(length_profile(amount, total, most, lean), jnp.int32)
    twos = (amount - 1) // 2
    giver, taker = tallies[1:1 + 2 * twos:2], tallies[2:2 + 2 * twos:2]
    room = jnp.minimum(giver - 1, most - taker)
    moved = jax.random.randint(jax.random.fold_in(stream_key, 1), (twos,), 0, 1 << 20) % (room + 1)
    tallies = tallies.at[1:1 + 2 * twos:2].set(giver - moved).at[2:2 + 2 * twos:2].set(taker + moved)
    return tallies[jax.random.permutation(jax.random.fold_in(stream_key, 2), amount)]


def normal_values(stream_key, extent, spread, most, cuts=(), held_as=jnp.bfloat16):
    loudness = block_levels(stream_key, extent, cuts, -0.22, 0.18) if cuts else 1.0
    drawn = jax.random.normal(stream_key, extent, jnp.float32) * spread * loudness
    return jnp.minimum(jnp.maximum(drawn, -most), most).astype(held_as)


def setup_inputs(seed: int = 0) -> dict:
    key_of = jax.random.split(jax.random.key(seed), 7)
    return {
        "guess": normal_values(key_of[0], (NSEC * CAP, RB), 1.0, 6.0, ((0, 8),), jnp.float32),
        "left_env": normal_values(key_of[1], (TERMS, NSEC * CAP, CAP), CAP ** -0.5, 0.21875, ((0, 4), (1, 8))),
        "right_env": normal_values(key_of[2], (TERMS, NSEC * RB, RB), RB ** -0.5, 0.375, ((0, 4), (1, 8))),
        "block_rows": ragged(key_of[3], NSEC, MEAN * NSEC, CAP, 2).astype(jnp.int32),
        "charges": draw_charges(jax.random.fold_in(key_of[6], 71), 0),
        "ranks": place_ends(jax.random.randint(key_of[5], (NSEC,), 1, RB + 1), jax.random.fold_in(key_of[5], 1), 1, RB).astype(jnp.int32),
    }


epsilon = 1e-06
step_size = 0.1
highest = lax.Precision.HIGHEST

def apply_operator(current, left_blocks, right_blocks, charges, row_mask):
    rounded = current.astype(jnp.bfloat16)

    def add_term(running, inputs):
        left_term, right_term, charge = inputs
        shifted = jnp.roll(rounded, charge, axis=0)
        middle = jnp.einsum('sij,sjk->sik', left_term.astype(jnp.float32), shifted.astype(jnp.float32)).astype(jnp.bfloat16)
        summand = jnp.einsum('sik,skl->sil', middle.astype(jnp.float32), right_term.astype(jnp.float32))
        return (running + summand, None)
    applied, unused = lax.scan(add_term, jnp.zeros(current.shape, jnp.float32), (left_blocks, right_blocks, charges))
    return applied * row_mask

def solve_block(lower_factor, right_side):
    return jax.scipy.linalg.cho_solve((lower_factor, True), right_side.T).T

def reference(guess, left_env, right_env, block_rows, charges, ranks):
    entries = MEAN * NSEC * RB
    positions = jnp.arange(CAP, dtype=jnp.int32)
    row_mask = (positions[None, :] < block_rows[:, None]).astype(jnp.float32)[:, :, None]
    current = guess.reshape(NSEC, CAP, RB) * row_mask
    current = current * lax.rsqrt(jnp.sum(current * current) / entries + epsilon)
    left_blocks = left_env.reshape(TERMS, NSEC, CAP, CAP)
    right_blocks = right_env.reshape(TERMS, NSEC, RB, RB)
    for repeat in range(ITERS):
        applied = apply_operator(current, left_blocks, right_blocks, charges.astype(jnp.int32), row_mask)
        rayleigh = jnp.sum(current * applied) / (jnp.sum(current * current) + epsilon)
        update = current - step_size * (applied - rayleigh * current)
        current = update * lax.rsqrt(jnp.sum(update * update) / entries + epsilon)
    density = jnp.einsum('sij,sik->sjk', current, current, precision=highest)
    columns = (jnp.arange(RB, dtype=jnp.int32)[None, :] < ranks[:, None]).astype(jnp.float32)
    span_basis = (jnp.eye(RB, dtype=jnp.float32)[None] + density / MEAN) * columns[:, None, :]
    gram_matrix = jnp.einsum('sij,sik->sjk', span_basis, span_basis, precision=highest) + jax.vmap(jnp.diag)(1.0 - columns)
    factor = jnp.linalg.cholesky(gram_matrix)
    coords = jnp.einsum('sij,sjk->sik', current, span_basis, precision=highest)
    solved = jax.vmap(solve_block)(factor, coords)
    truncated = jnp.einsum('sik,sjk->sij', solved, span_basis, precision=highest)
    return (current.reshape(NSEC * CAP, RB), truncated.reshape(NSEC * CAP, RB))
```

```python
import functools

import jax
import jax.numpy as jnp
from jax import lax
from jax.experimental import pallas as pl
from jax.experimental.pallas import tpu as pltpu
from jax.sharding import PartitionSpec as P

MEAN = 256
ITERS = 4


epsilon = 1e-06
step_size = 0.1
highest = lax.Precision.HIGHEST


def tile_sum(values):
    return jnp.sum(values.reshape(-1, 8, 128), axis=0)


def total(tile):
    return jnp.sum(jnp.sum(tile, axis=0, keepdims=True), axis=1, keepdims=True)


def iterate_kernel(
    sectors, members, entries,
    block_rows, charges, guess, left_hbm, right_hbm, out,
    left, right, xbuf, acc, app_chunk, cur, rs_out, rs_in, scal,
    load_sem, z_s, z_r, p_s, p_r, f_s, f_r, rs_s, rs_r, sc_s, sc_r,
):
    sector = lax.axis_index("sec")
    member = lax.axis_index("mpo")
    parity = lax.rem(sector, 2)
    capacity, width = guess.shape
    chunk = capacity // members
    terms = left.shape[0]
    sibling = sector + 1 - 2 * parity
    ahead = lax.rem(sector + 2, sectors)
    behind = lax.rem(sector + sectors - 2, sectors)
    sends = []

    loads = [
        pltpu.make_async_copy(left_hbm, left, load_sem.at[0]),
        pltpu.make_async_copy(right_hbm, right, load_sem.at[1]),
    ]
    for load in loads:
        load.start()

    barrier = pltpu.get_barrier_semaphore()
    for d in range(1, sectors):
        pl.semaphore_signal(
            barrier, inc=1, device_id=(lax.rem(sector + d, sectors), member),
            device_id_type=pl.DeviceIdType.MESH,
        )
    for d in range(1, members):
        pl.semaphore_signal(
            barrier, inc=1, device_id=(sector, lax.rem(member + d, members)),
            device_id_type=pl.DeviceIdType.MESH,
        )
    pl.semaphore_wait(barrier, sectors + members - 2)

    def remote(src, dst, send, recv, sec, mpo):
        return pltpu.make_async_remote_copy(
            src_ref=src, dst_ref=dst, send_sem=send, recv_sem=recv,
            device_id=(sec, mpo), device_id_type=pl.DeviceIdType.MESH,
        )

    def launch(copy):
        copy.start()
        sends.append(copy)

    def rows_of(j):
        return pl.ds(pl.multiple_of(j * chunk, chunk), chunk)

    def peer(d):
        return lax.rem(member + d, members)

    def z_copy(k, j, mpo):
        d = lax.rem(mpo - member + members, members)
        return remote(
            xbuf.at[k, 0, rows_of(j)], xbuf.at[k, 0, rows_of(j)],
            z_s.at[k, d], z_r.at[k, j], sector, mpo,
        )

    def plane_copy(k, j, slot):
        target = {1: sibling, 2: behind, 3: ahead}[slot]
        return remote(
            xbuf.at[k, 0, rows_of(j)], xbuf.at[k, slot, rows_of(j)],
            p_s.at[k, slot, j], p_r.at[k, slot, j], target, member,
        )

    def pass_copy(k, j):
        return remote(
            xbuf.at[k, 2 + parity, rows_of(j)], xbuf.at[k, 4, rows_of(j)],
            f_s.at[k, j], f_r.at[k, j], sibling, member,
        )

    def rs_copy(k, d):
        return remote(
            rs_out.at[k, d - 1], rs_in.at[k, d - 1],
            rs_s.at[k, d - 1], rs_r.at[k, d - 1], sector, peer(d),
        )

    def scal_copy(k, d):
        return remote(
            scal.at[k, sector], scal.at[k, sector],
            sc_s.at[k, d - 1], sc_r.at[k, d - 1], lax.rem(sector + d, sectors), member,
        )

    def scal_wait(k):
        for d in range(1, sectors):
            src = lax.rem(sector - d + sectors, sectors)
            remote(
                scal.at[k, src], scal.at[k, src],
                sc_s.at[k, d - 1], sc_r.at[k, d - 1], src, member,
            ).wait_recv()

    def plane_send(k, j):
        for slot in (2, 3, 1):
            launch(plane_copy(k, j, slot))

    def plane_wait(k, j, slot):
        remote(
            xbuf.at[k, slot, rows_of(j)], xbuf.at[k, slot, rows_of(j)],
            p_s.at[k, slot, j], p_r.at[k, slot, j], sibling, member,
        ).wait_recv()

    def other_wait(k, j):
        slot = 3 - parity
        remote(
            xbuf.at[k, slot, rows_of(j)], xbuf.at[k, slot, rows_of(j)],
            p_s.at[k, slot, j], p_r.at[k, slot, j], sibling, member,
        ).wait_recv()

    def passed_wait(k, j):
        slot = 2 + parity
        remote(
            xbuf.at[k, slot, rows_of(j)], xbuf.at[k, slot, rows_of(j)],
            p_s.at[k, slot, j], p_r.at[k, slot, j], sibling, member,
        ).wait_recv()

    def term_of(charge):
        index = jnp.int32(0)
        for i in range(1, terms):
            index = jnp.where(charges[i] == charge, i, index)
        return index

    slot_term = [
        term_of(0), term_of(2 * parity - 1), term_of(-2), term_of(2), term_of(1 - 2 * parity),
    ]

    def summand(k, slot, rows):
        index = slot_term[slot]
        middle = jnp.dot(
            left[index, rows, :], xbuf[k, slot], preferred_element_type=jnp.float32
        ).astype(jnp.bfloat16)
        return jnp.dot(middle, right[index], preferred_element_type=jnp.float32)

    def add_term(k, slot, first):
        def body(j, carry):
            rows = rows_of(j)
            value = summand(k, slot, rows)
            acc[rows, :] = value if first else acc[rows, :] + value
            return carry
        lax.fori_loop(0, members, body, 0)

    own_rows = block_rows[sector]
    order = [lax.rem(member + d, members) for d in range(members)]
    arrivals = [lax.rem(member - d + members, members) for d in range(members)]

    positions = lax.broadcasted_iota(jnp.int32, (capacity, width), 0)
    start = jnp.where(positions < own_rows, guess[...], 0.0)
    xbuf[0, 0] = start.astype(jnp.bfloat16)
    cur[...] = start
    for j in arrivals:
        plane_send(0, j)
    scal[0, sector, 0] = tile_sum(start * start)
    scal[0, sector, 1] = jnp.zeros((8, 128), jnp.float32)
    scal[0, sector, 2] = jnp.zeros((8, 128), jnp.float32)
    for d in range(1, sectors):
        launch(scal_copy(0, d))
    for load in loads:
        load.wait()

    def coefficients(k):
        sums = jnp.sum(scal[k], axis=0)
        if k == 0:
            scale = lax.rsqrt(total(sums[0]) / entries + epsilon)
            return scale, scale
        self_dot, cross_dot, image_dot = total(sums[0]), total(sums[1]), total(sums[2])
        rayleigh = cross_dot / (self_dot + epsilon)
        squares = self_dot * (1.0 - (step_size * rayleigh) ** 2) + step_size**2 * image_dot
        scale = lax.rsqrt(squares / entries + epsilon)
        return (1.0 + step_size * rayleigh) * scale, -step_size * scale

    for k in range(ITERS):
        last = k == ITERS - 1
        add_term(k, 0, True)
        for j in arrivals:
            plane_wait(k, j, 1)
        add_term(k, 1, False)
        for j in arrivals:
            passed_wait(k, j)
            launch(pass_copy(k, j))
        for j in arrivals:
            other_wait(k, j)
        add_term(k, 2, False)
        add_term(k, 3, False)
        for j in arrivals:
            remote(
                xbuf.at[k, 4, rows_of(j)], xbuf.at[k, 4, rows_of(j)],
                f_s.at[k, j], f_r.at[k, j], sibling, member,
            ).wait_recv()
        for d in range(1, members):
            rows = rows_of(order[d])
            rs_out[k, d - 1] = (acc[rows, :] + summand(k, 4, rows)).astype(jnp.bfloat16)
            launch(rs_copy(k, d))
        mine = rows_of(member)
        acc[mine, :] = acc[mine, :] + summand(k, 4, mine)
        scal_wait(k)
        keep, add = coefficients(k)
        for d in range(1, members):
            rs_copy(k, d).wait_recv()
        image = acc[mine, :]
        for d in range(1, members):
            image = image + rs_in[k, d - 1].astype(jnp.float32)
        positions = lax.broadcasted_iota(jnp.int32, (chunk, width), 0) + member * chunk
        image = jnp.where(positions < own_rows, image, 0.0) * add
        if k > 0:
            image = image + keep * app_chunk[...]
        app_chunk[...] = image
        xbuf[k + 1, 0, mine] = image.astype(jnp.bfloat16)
        for d in range(1, members):
            launch(z_copy(k + 1, member, order[d]))
        if not last:
            plane_send(k + 1, member)
        if k == 0:
            cur[...] = keep * cur[...]
        else:
            cur[...] = keep * cur[...] + add * xbuf[k, 0].astype(jnp.float32)
        for d in range(1, members):
            j = arrivals[d]
            remote(
                xbuf.at[k + 1, 0, rows_of(j)], xbuf.at[k + 1, 0, rows_of(j)],
                z_s.at[k + 1, d], z_r.at[k + 1, j], sector, order[d],
            ).wait_recv()
            if not last:
                plane_send(k + 1, j)
        state = cur[...]
        applied = xbuf[k + 1, 0].astype(jnp.float32)
        scal[k + 1, sector, 0] = tile_sum(state * state)
        scal[k + 1, sector, 1] = tile_sum(state * applied)
        scal[k + 1, sector, 2] = tile_sum(applied * applied)
        for d in range(1, sectors):
            launch(scal_copy(k + 1, d))
    scal_wait(ITERS)
    keep, add = coefficients(ITERS)
    out[...] = keep * cur[...] + add * xbuf[ITERS, 0].astype(jnp.float32)
    for copy in sends:
        copy.wait_send()


def iterate(guess, left_env, right_env, block_rows, charges):
    capacity, width = guess.shape
    terms = left_env.shape[0]
    sectors = lax.axis_size("sec")
    members = lax.axis_size("mpo")
    chunk = capacity // members
    entries = MEAN * sectors * width
    dma = pltpu.SemaphoreType.DMA
    vmem = pl.BlockSpec(memory_space=pltpu.VMEM)
    smem = pl.BlockSpec(memory_space=pltpu.SMEM)
    hbm = pl.BlockSpec(memory_space=pl.ANY)
    return pl.pallas_call(
        functools.partial(iterate_kernel, sectors, members, entries),
        out_shape=jax.ShapeDtypeStruct((capacity, width), jnp.float32),
        in_specs=[smem, smem, vmem, hbm, hbm],
        out_specs=vmem,
        scratch_shapes=[
            pltpu.VMEM(left_env.shape, left_env.dtype),
            pltpu.VMEM((terms, width, width), right_env.dtype),
            pltpu.VMEM((ITERS + 1, 5, capacity, width), jnp.bfloat16),
            pltpu.VMEM((capacity, width), jnp.float32),
            pltpu.VMEM((chunk, width), jnp.float32),
            pltpu.VMEM((capacity, width), jnp.float32),
            pltpu.VMEM((ITERS, members - 1, chunk, width), jnp.bfloat16),
            pltpu.VMEM((ITERS, members - 1, chunk, width), jnp.bfloat16),
            pltpu.VMEM((ITERS + 1, sectors, 3, 8, 128), jnp.float32),
            dma((2,)),
            dma((ITERS + 1, members)),
            dma((ITERS + 1, members)),
            dma((ITERS + 1, 5, members)),
            dma((ITERS + 1, 5, members)),
            dma((ITERS + 1, members)),
            dma((ITERS + 1, members)),
            dma((ITERS, members)),
            dma((ITERS, members)),
            dma((ITERS + 1, sectors)),
            dma((ITERS + 1, sectors)),
        ],
        compiler_params=pltpu.CompilerParams(
            collective_id=0, has_side_effects=True, vmem_limit_bytes=56 * 1024 * 1024
        ),
    )(block_rows, charges, guess, left_env, right_env)


def shards(guess, left_env, right_env, block_rows, charges, ranks):
    capacity, right_width = guess.shape
    sectors = block_rows.shape[0]
    sector = lax.axis_index("sec")
    member = lax.axis_index("mpo")
    members = lax.axis_size("mpo")
    slab_rows = capacity // members
    sector_ids = jnp.arange(sectors, dtype=jnp.int32)
    own_rank = jnp.sum(jnp.where(sector_ids == sector, ranks, 0))
    current = iterate(guess, left_env, right_env, block_rows, charges)
    density = jnp.einsum("ij,ik->jk", current, current, precision=highest)
    slab = lax.dynamic_slice_in_dim(current, member * slab_rows, slab_rows, 0)
    columns = (jnp.arange(right_width, dtype=jnp.int32) < own_rank).astype(jnp.float32)
    span_basis = (jnp.eye(right_width, dtype=jnp.float32) + density / MEAN) * columns[None, :]
    gram_matrix = jnp.einsum("ij,ik->jk", span_basis, span_basis, precision=highest) + jnp.diag(
        1.0 - columns
    )
    factor = jnp.linalg.cholesky(gram_matrix)
    coords = jnp.einsum("ij,jk->ik", slab, span_basis, precision=highest)
    solved = jax.scipy.linalg.cho_solve((factor, True), coords.T).T
    truncated = jnp.einsum("ik,jk->ij", solved, span_basis, precision=highest)
    return (slab, truncated)


def solution(mesh):
    return jax.shard_map(
        shards,
        mesh=mesh,
        in_specs=(P("sec", None), P("mpo", "sec", None), P("mpo", "sec", None), P(), P("mpo"), P()),
        out_specs=(P(("sec", "mpo"), None), P(("sec", "mpo"), None)),
        check_vma=False,
    )
```

```python
import functools

import jax
import jax.numpy as jnp
from jax import lax
from jax.experimental import pallas as pl
from jax.experimental.pallas import tpu as pltpu
from jax.sharding import PartitionSpec as P

MEAN = 256
ITERS = 4


epsilon = 1e-06
step_size = 0.1
highest = lax.Precision.HIGHEST


def tile_sum(values):
    return jnp.sum(values.reshape(-1, 8, 128), axis=0)


def total(tile):
    return jnp.sum(jnp.sum(tile, axis=0, keepdims=True), axis=1, keepdims=True)


def iterate_kernel(
    sectors, members, entries,
    block_rows, charges, guess, left_hbm, right_hbm, out,
    left, right, xbuf, acc, app_chunk, cur, rs_out, rs_in, scal,
    load_sem, z_s, z_r, p_s, p_r, f_s, f_r, rs_s, rs_r, sc_s, sc_r,
):
    sector = lax.axis_index("sec")
    member = lax.axis_index("mpo")
    parity = lax.rem(sector, 2)
    capacity, width = guess.shape
    chunk = capacity // members
    terms = left.shape[0]
    sibling = sector + 1 - 2 * parity
    ahead = lax.rem(sector + 2, sectors)
    behind = lax.rem(sector + sectors - 2, sectors)
    sends = []

    loads = [
        pltpu.make_async_copy(left_hbm, left, load_sem.at[0]),
        pltpu.make_async_copy(right_hbm, right, load_sem.at[1]),
    ]
    for load in loads:
        load.start()

    barrier = pltpu.get_barrier_semaphore()
    for d in range(1, sectors):
        pl.semaphore_signal(
            barrier, inc=1, device_id=(lax.rem(sector + d, sectors), member),
            device_id_type=pl.DeviceIdType.MESH,
        )
    for d in range(1, members):
        pl.semaphore_signal(
            barrier, inc=1, device_id=(sector, lax.rem(member + d, members)),
            device_id_type=pl.DeviceIdType.MESH,
        )
    pl.semaphore_wait(barrier, sectors + members - 2)

    def remote(src, dst, send, recv, sec, mpo):
        return pltpu.make_async_remote_copy(
            src_ref=src, dst_ref=dst, send_sem=send, recv_sem=recv,
            device_id=(sec, mpo), device_id_type=pl.DeviceIdType.MESH,
        )

    def launch(copy):
        copy.start()
        sends.append(copy)

    def rows_of(j):
        return pl.ds(pl.multiple_of(j * chunk, chunk), chunk)

    def peer(d):
        return lax.rem(member + d, members)

    def z_copy(k, j, mpo):
        d = lax.rem(mpo - member + members, members)
        return remote(
            xbuf.at[k, 0, rows_of(j)], xbuf.at[k, 0, rows_of(j)],
            z_s.at[k, d], z_r.at[k, j], sector, mpo,
        )

    def plane_copy(k, j, slot):
        target = {1: sibling, 2: behind, 3: ahead}[slot]
        return remote(
            xbuf.at[k, 0, rows_of(j)], xbuf.at[k, slot, rows_of(j)],
            p_s.at[k, slot, j], p_r.at[k, slot, j], target, member,
        )

    def pass_copy(k, j):
        return remote(
            xbuf.at[k, 2 + parity, rows_of(j)], xbuf.at[k, 4, rows_of(j)],
            f_s.at[k, j], f_r.at[k, j], sibling, member,
        )

    def rs_copy(k, d):
        return remote(
            rs_out.at[k, d - 1], rs_in.at[k, d - 1],
            rs_s.at[k, d - 1], rs_r.at[k, d - 1], sector, peer(d),
        )

    def scal_copy(k, d):
        return remote(
            scal.at[k, sector], scal.at[k, sector],
            sc_s.at[k, d - 1], sc_r.at[k, d - 1], lax.rem(sector + d, sectors), member,
        )

    def scal_wait(k):
        for d in range(1, sectors):
            src = lax.rem(sector - d + sectors, sectors)
            remote(
                scal.at[k, src], scal.at[k, src],
                sc_s.at[k, d - 1], sc_r.at[k, d - 1], src, member,
            ).wait_recv()

    def plane_send(k, j):
        for slot in (2, 3, 1):
            launch(plane_copy(k, j, slot))

    def plane_wait(k, j, slot):
        remote(
            xbuf.at[k, slot, rows_of(j)], xbuf.at[k, slot, rows_of(j)],
            p_s.at[k, slot, j], p_r.at[k, slot, j], sibling, member,
        ).wait_recv()

    def other_wait(k, j):
        slot = 3 - parity
        remote(
            xbuf.at[k, slot, rows_of(j)], xbuf.at[k, slot, rows_of(j)],
            p_s.at[k, slot, j], p_r.at[k, slot, j], sibling, member,
        ).wait_recv()

    def passed_wait(k, j):
        slot = 2 + parity
        remote(
            xbuf.at[k, slot, rows_of(j)], xbuf.at[k, slot, rows_of(j)],
            p_s.at[k, slot, j], p_r.at[k, slot, j], sibling, member,
        ).wait_recv()

    def term_of(charge):
        index = jnp.int32(0)
        for i in range(1, terms):
            index = jnp.where(charges[i] == charge, i, index)
        return index

    slot_term = [
        term_of(0), term_of(2 * parity - 1), term_of(-2), term_of(2), term_of(1 - 2 * parity),
    ]

    def summand(k, slot, rows):
        index = slot_term[slot]
        middle = jnp.dot(
            left[index, rows, :], xbuf[k, slot], preferred_element_type=jnp.float32
        ).astype(jnp.bfloat16)
        return jnp.dot(middle, right[index], preferred_element_type=jnp.float32)

    def add_term(k, slot, first):
        def body(j, carry):
            rows = rows_of(j)
            value = summand(k, slot, rows)
            acc[rows, :] = value if first else acc[rows, :] + value
            return carry
        lax.fori_loop(0, members, body, 0)

    own_rows = block_rows[sector]
    order = [lax.rem(member + d, members) for d in range(members)]
    arrivals = [lax.rem(member - d + members, members) for d in range(members)]

    positions = lax.broadcasted_iota(jnp.int32, (capacity, width), 0)
    start = jnp.where(positions < own_rows, guess[...], 0.0)
    xbuf[0, 0] = start.astype(jnp.bfloat16)
    cur[...] = start
    for j in arrivals:
        plane_send(0, j)
    scal[0, sector, 0] = tile_sum(start * start)
    scal[0, sector, 1] = jnp.zeros((8, 128), jnp.float32)
    scal[0, sector, 2] = jnp.zeros((8, 128), jnp.float32)
    for d in range(1, sectors):
        launch(scal_copy(0, d))
    for load in loads:
        load.wait()

    def coefficients(k):
        sums = jnp.sum(scal[k], axis=0)
        if k == 0:
            scale = lax.rsqrt(total(sums[0]) / entries + epsilon)
            return scale, scale
        self_dot, cross_dot, image_dot = total(sums[0]), total(sums[1]), total(sums[2])
        rayleigh = cross_dot / (self_dot + epsilon)
        squares = self_dot * (1.0 - (step_size * rayleigh) ** 2) + step_size**2 * image_dot
        scale = lax.rsqrt(squares / entries + epsilon)
        return (1.0 + step_size * rayleigh) * scale, -step_size * scale

    for k in range(ITERS):
        last = k == ITERS - 1
        add_term(k, 0, True)
        for j in arrivals:
            plane_wait(k, j, 1)
        add_term(k, 1, False)
        for j in arrivals:
            passed_wait(k, j)
            launch(pass_copy(k, j))
        for j in arrivals:
            other_wait(k, j)
        add_term(k, 2, False)
        add_term(k, 3, False)
        for j in arrivals:
            remote(
                xbuf.at[k, 4, rows_of(j)], xbuf.at[k, 4, rows_of(j)],
                f_s.at[k, j], f_r.at[k, j], sibling, member,
            ).wait_recv()
        for d in range(1, members):
            rows = rows_of(order[d])
            rs_out[k, d - 1] = (acc[rows, :] + summand(k, 4, rows)).astype(jnp.bfloat16)
            launch(rs_copy(k, d))
        mine = rows_of(member)
        acc[mine, :] = acc[mine, :] + summand(k, 4, mine)
        scal_wait(k)
        keep, add = coefficients(k)
        for d in range(1, members):
            rs_copy(k, d).wait_recv()
        image = acc[mine, :]
        for d in range(1, members):
            image = image + rs_in[k, d - 1].astype(jnp.float32)
        positions = lax.broadcasted_iota(jnp.int32, (chunk, width), 0) + member * chunk
        image = jnp.where(positions < own_rows, image, 0.0) * add
        if k > 0:
            image = image + keep * app_chunk[...]
        app_chunk[...] = image
        xbuf[k + 1, 0, mine] = image.astype(jnp.bfloat16)
        for d in range(1, members):
            launch(z_copy(k + 1, member, order[d]))
        if not last:
            plane_send(k + 1, member)
        if k == 0:
            cur[...] = keep * cur[...]
        else:
            cur[...] = keep * cur[...] + add * xbuf[k, 0].astype(jnp.float32)
        for d in range(1, members):
            j = arrivals[d]
            remote(
                xbuf.at[k + 1, 0, rows_of(j)], xbuf.at[k + 1, 0, rows_of(j)],
                z_s.at[k + 1, d], z_r.at[k + 1, j], sector, order[d],
            ).wait_recv()
            if not last:
                plane_send(k + 1, j)
        state = cur[...]
        applied = xbuf[k + 1, 0].astype(jnp.float32)
        scal[k + 1, sector, 0] = tile_sum(state * state)
        scal[k + 1, sector, 1] = tile_sum(state * applied)
        scal[k + 1, sector, 2] = tile_sum(applied * applied)
        for d in range(1, sectors):
            launch(scal_copy(k + 1, d))
    scal_wait(ITERS)
    keep, add = coefficients(ITERS)
    out[...] = keep * cur[...] + add * xbuf[ITERS, 0].astype(jnp.float32)
    for copy in sends:
        copy.wait_send()


def iterate(guess, left_env, right_env, block_rows, charges):
    capacity, width = guess.shape
    terms = left_env.shape[0]
    sectors = lax.axis_size("sec")
    members = lax.axis_size("mpo")
    chunk = capacity // members
    entries = MEAN * sectors * width
    dma = pltpu.SemaphoreType.DMA
    vmem = pl.BlockSpec(memory_space=pltpu.VMEM)
    smem = pl.BlockSpec(memory_space=pltpu.SMEM)
    hbm = pl.BlockSpec(memory_space=pl.ANY)
    return pl.pallas_call(
        functools.partial(iterate_kernel, sectors, members, entries),
        out_shape=jax.ShapeDtypeStruct((capacity, width), jnp.float32),
        in_specs=[smem, smem, vmem, hbm, hbm],
        out_specs=vmem,
        scratch_shapes=[
            pltpu.VMEM(left_env.shape, left_env.dtype),
            pltpu.VMEM((terms, width, width), right_env.dtype),
            pltpu.VMEM((ITERS + 1, 5, capacity, width), jnp.bfloat16),
            pltpu.VMEM((capacity, width), jnp.float32),
            pltpu.VMEM((chunk, width), jnp.float32),
            pltpu.VMEM((capacity, width), jnp.float32),
            pltpu.VMEM((ITERS, members - 1, chunk, width), jnp.bfloat16),
            pltpu.VMEM((ITERS, members - 1, chunk, width), jnp.bfloat16),
            pltpu.VMEM((ITERS + 1, sectors, 3, 8, 128), jnp.float32),
            dma((2,)),
            dma((ITERS + 1, members)),
            dma((ITERS + 1, members)),
            dma((ITERS + 1, 5, members)),
            dma((ITERS + 1, 5, members)),
            dma((ITERS + 1, members)),
            dma((ITERS + 1, members)),
            dma((ITERS, members)),
            dma((ITERS, members)),
            dma((ITERS + 1, sectors)),
            dma((ITERS + 1, sectors)),
        ],
        compiler_params=pltpu.CompilerParams(
            collective_id=0, has_side_effects=True, vmem_limit_bytes=56 * 1024 * 1024
        ),
    )(block_rows, charges, guess, left_env, right_env)


BLOCK = 64


def exact_dot(left, right, dims):
    return lax.dot_general(
        left, right, (dims, ((), ())), precision=highest, preferred_element_type=jnp.float32
    )


def inverse_factor(block):
    rows = lax.broadcasted_iota(jnp.int32, (BLOCK, BLOCK), 0)
    lanes = lax.broadcasted_iota(jnp.int32, (BLOCK, BLOCK), 1)
    joined = jnp.concatenate([block, jnp.where(rows == lanes, 1.0, 0.0)], axis=1)
    tiles = [joined[8 * i:8 * i + 8, :] for i in range(BLOCK // 8)]
    below = lax.broadcasted_iota(jnp.int32, (8, 1), 0)
    for j in range(BLOCK):
        home, offset = divmod(j, 8)
        row = tiles[home][offset:offset + 1, :]
        scaled = row / row[:, j:j + 1]
        for i in range(home, BLOCK // 8):
            column = tiles[i][:, j:j + 1]
            if i == home:
                if offset == 7:
                    continue
                column = jnp.where(below > offset, column, 0.0)
            tiles[i] = tiles[i] - column * scaled
    joined = jnp.concatenate(tiles, axis=0)
    wide_rows = lax.broadcasted_iota(jnp.int32, joined.shape, 0)
    wide_lanes = lax.broadcasted_iota(jnp.int32, joined.shape, 1)
    pivots = jnp.sum(jnp.where(wide_rows == wide_lanes, joined, 0.0), axis=1, keepdims=True)
    return (joined * lax.rsqrt(pivots))[:, BLOCK:]


def truncate_kernel(rank, density, slab, out, work, solved):
    width = density.shape[0]
    rows = lax.broadcasted_iota(jnp.int32, (width, width), 0)
    lanes = lax.broadcasted_iota(jnp.int32, (width, width), 1)
    identity = jnp.where(rows == lanes, 1.0, 0.0)
    full = identity + density[...] / MEAN
    kept = rank[0]
    basis = jnp.where(lanes < kept, full, 0.0)
    basis_t = jnp.where(rows < kept, full, 0.0)
    work[:, :width] = exact_dot(basis_t, basis, ((1,), (0,))) + jnp.where(
        rows < kept, 0.0, identity
    )
    work[:, width:] = basis_t
    for first in range(0, width, BLOCK):
        rest = first + BLOCK
        inverse = inverse_factor(work[first:rest, first:rest])
        reduced = exact_dot(inverse, work[first:rest, :], ((1,), (0,)))
        solved[first:rest, :] = reduced[:, width:]
        if rest < width:
            column = exact_dot(work[rest:, first:rest], inverse, ((1,), (1,)))
            work[rest:, :] = work[rest:, :] - exact_dot(column, reduced, ((1,), (0,)))
    coords = exact_dot(slab[...], solved[...], ((1,), (1,)))
    out[...] = exact_dot(coords, solved[...], ((1,), (0,)))


def truncate(density, slab, rank):
    width = density.shape[0]
    vmem = pl.BlockSpec(memory_space=pltpu.VMEM)
    return pl.pallas_call(
        truncate_kernel,
        out_shape=jax.ShapeDtypeStruct(slab.shape, jnp.float32),
        in_specs=[pl.BlockSpec(memory_space=pltpu.SMEM), vmem, vmem],
        out_specs=vmem,
        scratch_shapes=[
            pltpu.VMEM((width, 2 * width), jnp.float32),
            pltpu.VMEM((width, width), jnp.float32),
        ],
    )(rank, density, slab)


def shards(guess, left_env, right_env, block_rows, charges, ranks):
    capacity, right_width = guess.shape
    sectors = block_rows.shape[0]
    sector = lax.axis_index("sec")
    member = lax.axis_index("mpo")
    members = lax.axis_size("mpo")
    slab_rows = capacity // members
    sector_ids = jnp.arange(sectors, dtype=jnp.int32)
    own_rank = jnp.sum(jnp.where(sector_ids == sector, ranks, 0))
    current = iterate(guess, left_env, right_env, block_rows, charges)
    density = jnp.einsum("ij,ik->jk", current, current, precision=highest)
    slab = lax.dynamic_slice_in_dim(current, member * slab_rows, slab_rows, 0)
    truncated = truncate(density, slab, own_rank.reshape(1))
    return (slab, truncated)


def solution(mesh):
    return jax.shard_map(
        shards,
        mesh=mesh,
        in_specs=(P("sec", None), P("mpo", "sec", None), P("mpo", "sec", None), P(), P("mpo"), P()),
        out_specs=(P(("sec", "mpo"), None), P(("sec", "mpo"), None)),
        check_vma=False,
    )
```
